32 devices in a mesh: dp: 4 (over z), ctx: 8 (over y, x, core).
Axes of the slice: x: 2, y: 2, z: 4, core: 2. Of those that a mesh axis runs over, the one named last changes fastest.
Arguments:
- patches: bfloat16 [8, 1024, 6144], P('dp', 'ctx'), may hold values from -6 to 6
- w_in: bfloat16 [6144, 768], P(('dp', 'ctx')), may hold values from -0.078125 to 0.078125
- b_in: bfloat16 [768], P(('dp', 'ctx')), may hold values from -3 to 3
- g_one: bfloat16 [768], P(('dp', 'ctx')), may hold values from 0.25 to 1.75
- s_one: bfloat16 [768], P(('dp', 'ctx')), may hold values from -3 to 3
- w_qkv: bfloat16 [768, 2304], P(('dp', 'ctx')), may hold values from -0.21875 to 0.21875
- w_out: bfloat16 [768, 768], P(('dp', 'ctx')), may hold values from -1.75 to 1.75
- b_out: bfloat16 [768], P(('dp', 'ctx')), may hold values from -3 to 3
- g_two: bfloat16 [768], P(('dp', 'ctx')), may hold values from 0.25 to 1.75
- s_two: bfloat16 [768], P(('dp', 'ctx')), may hold values from -3 to 3
- w_up: bfloat16 [768, 3072], P(('dp', 'ctx')), may hold values from -0.21875 to 0.21875
- b_up: bfloat16 [3072], P(('dp', 'ctx')), may hold values from -3 to 3
- w_down: bfloat16 [3072, 768], P(('dp', 'ctx')), may hold values from -0.109375 to 0.109375
- b_down: bfloat16 [768], P(('dp', 'ctx')), may hold values from -3 to 3
- cotangent: bfloat16 [8, 1024, 768], P('dp', 'ctx'), may hold values from -6 to 6
Outputs:
- block_out: bfloat16 [8, 1024, 768], P('dp', 'ctx')
- grad_patches: float32 [8, 1024, 6144], P('dp', 'ctx')
- grad_w_in: float32 [6144, 768], P(('dp', 'ctx'))
- grad_b_in: float32 [768], P(('dp', 'ctx'))
- grad_g_one: float32 [768], P(('dp', 'ctx'))
- grad_s_one: float32 [768], P(('dp', 'ctx'))
- grad_w_qkv: float32 [768, 2304], P(('dp', 'ctx'))
- grad_w_out: float32 [768, 768], P(('dp', 'ctx'))
- grad_b_out: float32 [768], P(('dp', 'ctx'))
- grad_g_two: float32 [768], P(('dp', 'ctx'))
- grad_s_two: float32 [768], P(('dp', 'ctx'))
- grad_w_up: float32 [768, 3072], P(('dp', 'ctx'))
- grad_b_up: float32 [3072], P(('dp', 'ctx'))
- grad_w_down: float32 [3072, 768], P(('dp', 'ctx'))
- grad_b_down: float32 [768], P(('dp', 'ctx'))
The draws below stay inside these ranges and needn't reach their ends.
All inputs are finite; a program needn't handle non-finite values.
Results may differ from the reference program's by a relative error of at most 0.015.
Values may be sent and summed in bfloat16 or wider, within the bound.
No kernel may reach another device: no remote copies, remote signals or barrier semaphores. Data moves between devices by JAX's collectives and lax.ppermute only.
A program may use at most 256 MiB of HBM per device.

```python
import jax
import jax.numpy as jnp
from jax import lax

D = 768
HEADS = 12
HEAD = 64
FF = 3072
IN = 6144
LENGTH = 1024
SEQS = 8


def raised(values, rng, source, target, parts, factor):
    owner, partner = [(jnp.arange(values.shape[dim]) // (values.shape[dim] // parts)).reshape([-1 if axis == dim else 1 for axis in range(values.ndim)]) for dim in (source, target)]
    chosen = jax.random.permutation(rng, parts)[partner]
    strong = (owner == chosen) | (owner == (partner + parts // 2) % parts)
    return jnp.where(strong, factor * values, values)


def steps_of(rng, dims, split, least, top_value):
    def one(position, blocks):
        steps = jax.random.uniform(jax.random.fold_in(jax.random.fold_in(rng, 6), position), (blocks,), jnp.float32, least / len(split), top_value / len(split))
        return jnp.repeat(jnp.exp(steps), dims[position] // blocks).reshape((-1,) + (1,) * (len(dims) - position - 1))

    level = one(*split[0])
    for cut in split[1:]:
        level = level * one(*cut)
    return level


def centred(key, dims, deviation, limit, shards=(), kind=jnp.bfloat16):
    array = jax.random.normal(key, dims, jnp.float32) * deviation
    if len(shards) > 0:
        array = steps_of(key, dims, shards, -0.22, 0.18) * array
    return jnp.clip(array, min=-limit, max=limit).astype(kind)


def gaussian_with(stream_key, shape, width, most, cuts, heavy, held_as=jnp.bfloat16):
    values = width * jax.random.normal(stream_key, shape, jnp.float32)
    if cuts:
        values = values * steps_of(stream_key, shape, cuts, -0.22, 0.18)
    return jnp.clip(raised(values, jax.random.fold_in(stream_key, 3), *heavy), -most, most).astype(held_as)


def setup_inputs(seed: int = 0) -> dict:
    keys = jax.random.split(jax.random.key(seed), 16)
    return {
        "patches": gaussian_with(keys[0], (SEQS, LENGTH, IN), 1.0, 6.0, ((0, 4), (1, 8)), (1, 2, 8, 2.0)),
        "w_in": centred(keys[1], (IN, D), IN ** -0.5, 0.078125, ((0, 32),)),
        "b_in": centred(keys[2], (D,), 0.5, 3.0, ((0, 32),)),
        "g_one": jnp.clip(1.0 + 0.15 * jax.random.normal(keys[3], (D,), jnp.float32), 0.25, 1.75).astype(jnp.bfloat16),
        "s_one": centred(keys[4], (D,), 0.5, 3.0, ((0, 32),)),
        "w_qkv": centred(keys[5], (D, 3 * D), D ** -0.5, 0.21875, ((0, 32),)),
        "w_out": centred(keys[6], (D, D), (max(1, D * 16 // LENGTH)) ** -0.5, 1.75, ((0, 32),)),
        "b_out": centred(keys[7], (D,), 0.5, 3.0, ((0, 32),)),
        "g_two": jnp.clip(1.0 + 0.15 * jax.random.normal(keys[8], (D,), jnp.float32), 0.25, 1.75).astype(jnp.bfloat16),
        "s_two": centred(keys[9], (D,), 0.5, 3.0, ((0, 32),)),
        "w_up": centred(keys[10], (D, FF), D ** -0.5, 0.21875, ((0, 32),)),
        "b_up": centred(keys[11], (FF,), 0.5, 3.0, ((0, 32),)),
        "w_down": centred(keys[12], (FF, D), FF ** -0.5, 0.109375, ((0, 32),)),
        "b_down": centred(keys[13], (D,), 0.5, 3.0, ((0, 32),)),
        "cotangent": gaussian_with(keys[14], (SEQS, LENGTH, D), 1.0, 6.0, ((0, 4), (1, 8)), (1, 2, 8, 2.0)),
    }


@jax.custom_vjp
def low(v):
    return lax.optimization_barrier(v.astype(jnp.bfloat16)).astype(jnp.float32)

@jax.custom_vjp
def low_back(v):
    return v

def low_keep(v):
    return (low(v), None)

def low_pass(kept, grad):
    return (grad,)

def back_keep(v):
    return (v, None)

def back_low(kept, grad):
    return (low(grad),)
low.defvjp(low_keep, low_pass)
low_back.defvjp(back_keep, back_low)
eps_norm = 1e-05
gelu_coef = 0.7978845608028654

def matmul(left, right):
    return jnp.dot(left, right, precision=lax.Precision.HIGHEST, preferred_element_type=jnp.float32)

def layer_norm(stream, gain, shift):
    row_mean = lax.optimization_barrier(jnp.mean(stream, axis=-1, keepdims=True))
    centered = stream - row_mean
    variance = lax.optimization_barrier(jnp.mean(centered * centered, axis=-1, keepdims=True))
    return centered * lax.rsqrt(variance + eps_norm) * gain + shift

def gelu_tanh(pre_act):
    return 0.5 * pre_act * (1.0 + jnp.tanh(gelu_coef * (pre_act + 0.044715 * pre_act * pre_act * pre_act)))

def block_forward(seq_patches, params):
    w_in, b_in, g_one, s_one, w_qkv, w_out, b_out, g_two, s_two, w_up, b_up, w_down, b_down = params
    h_zero = low_back(matmul(seq_patches, w_in)) + b_in
    a_one = low(layer_norm(h_zero, g_one, s_one))
    projected = low(low_back(matmul(a_one, w_qkv)))
    length = projected.shape[0]
    queries = projected[:, :D].reshape(length, HEADS, HEAD)
    key_rows = projected[:, D:2 * D].reshape(length, HEADS, HEAD)
    value_rows = projected[:, 2 * D:].reshape(length, HEADS, HEAD)
    query_width = min(512, length)
    blocks = length // query_width
    query_blocks = queries.reshape(blocks, query_width, HEADS, HEAD)
    offsets = jnp.arange(blocks, dtype=jnp.int32) * query_width

    def attend(entry):
        query_block, offset = entry
        raw = jnp.einsum('qhd,khd->hqk', query_block, key_rows, precision=lax.Precision.HIGHEST)
        scores = low_back(raw * 0.125)
        row_pos = offset + jnp.arange(query_width, dtype=jnp.int32)
        key_pos = jnp.arange(length, dtype=jnp.int32)
        allowed = key_pos[None, :] <= row_pos[:, None]
        scores = jnp.where(allowed[None], scores, -1e+30)
        row_top = lax.optimization_barrier(jnp.max(scores, axis=-1, keepdims=True))
        expon = jnp.exp(scores - row_top)
        attn_probs = low(expon / lax.optimization_barrier(jnp.sum(expon, axis=-1, keepdims=True)))
        return jnp.einsum('hqk,khd->qhd', attn_probs, value_rows, precision=lax.Precision.HIGHEST)
    attended = lax.map(jax.checkpoint(attend), (query_blocks, offsets)).reshape(length, D)
    attended = low(low_back(attended))
    h_one = h_zero + low_back(matmul(attended, w_out)) + b_out
    a_two = low(layer_norm(h_one, g_two, s_two))
    hidden = low(gelu_tanh(low_back(matmul(a_two, w_up)) + b_up))
    return h_one + low_back(matmul(hidden, w_down)) + b_down

def reference(patches, w_in, b_in, g_one, s_one, w_qkv, w_out, b_out, g_two, s_two, w_up, b_up, w_down, b_down, cotangent):
    params = tuple((weight.astype(jnp.float32) for weight in (w_in, b_in, g_one, s_one, w_qkv, w_out, b_out, g_two, s_two, w_up, b_up, w_down, b_down)))

    def one_sequence(totals, entry):
        seq_patches, seq_cot = entry
        result, pull = jax.vjp(block_forward, seq_patches.astype(jnp.float32), params)
        grad_input, grad_params = pull(seq_cot.astype(jnp.float32))
        totals = jax.tree.map(lambda first, second: first + second, totals, grad_params)
        return (totals, (result.astype(jnp.bfloat16), grad_input))
    zeros = tuple((jnp.zeros_like(weight) for weight in params))
    totals, (outputs, grad_inputs) = lax.scan(one_sequence, zeros, (patches, cotangent))
    return (outputs, grad_inputs, totals[0], totals[1], totals[2], totals[3], totals[4], totals[5], totals[6], totals[7], totals[8], totals[9], totals[10], totals[11], totals[12])
```

```python
import math

import jax
import jax.numpy as jnp
import numpy as np
from jax import lax
from jax.experimental import pallas as pl
from jax.experimental.pallas import tpu as pltpu
from jax.sharding import Mesh
from jax.sharding import PartitionSpec as P

HEADS = 12
HEAD = 64

eps_norm = 1e-05
gelu_coef = 0.7978845608028654
PLANE = ("y", "x", "c")
ALL = ("z", "y", "x", "c")
bf16 = jnp.bfloat16
f32 = jnp.float32


def norm_forward(stream, gain, shift):
    row_mean = jnp.mean(stream, axis=-1, keepdims=True)
    centered = stream - row_mean
    variance = jnp.mean(centered * centered, axis=-1, keepdims=True)
    inverse = lax.rsqrt(variance + eps_norm)
    normed = centered * inverse
    return (normed * gain + shift, normed, inverse)


def norm_backward(upstream, normed, inverse, gain):
    scaled = upstream * gain
    row_inner = jnp.mean(scaled, axis=-1, keepdims=True)
    row_corr = jnp.mean(scaled * normed, axis=-1, keepdims=True)
    stream_grad = inverse * (scaled - row_inner - normed * row_corr)
    return (stream_grad, jnp.sum(upstream * normed, axis=0), jnp.sum(upstream, axis=0))


def gelu_pair(pre_act):
    tanh_val = jnp.tanh(gelu_coef * (pre_act + 0.044715 * pre_act * pre_act * pre_act))
    gelu_out = 0.5 * pre_act * (1.0 + tanh_val)
    gelu_slope = 0.5 * (1.0 + tanh_val) + 0.5 * pre_act * (
        1.0 - tanh_val * tanh_val
    ) * gelu_coef * (1.0 + 3.0 * 0.044715 * pre_act * pre_act)
    return (gelu_out, gelu_slope)


def dot(left, right):
    return jnp.dot(left, right, preferred_element_type=f32)


def dot_nt(left, right):
    return lax.dot_general(left, right, (((1,), (1,)), ((), ())), preferred_element_type=f32)


def dot_tn(left, right):
    return lax.dot_general(left, right, (((0,), (0,)), ((), ())), preferred_element_type=f32)


def swap(value, axis, step):
    size = lax.axis_size(axis)
    return lax.ppermute(value, axis, [(place, place ^ step) for place in range(size)])


def pick(value, index, dim=0):
    return lax.dynamic_index_in_dim(value, index, dim, keepdims=False)


def stacked_heads(block):
    lane = lax.broadcasted_iota(jnp.int32, block.shape, 1)
    zero = jnp.zeros_like(block)
    return jnp.concatenate(
        [jnp.where(lane < HEAD, block, zero), jnp.where(lane < HEAD, zero, block)], axis=0
    )


def masked_scores(places, keys, two_queries, slots, rows):
    scores = dot_nt(keys, two_queries)
    key_row = lax.broadcasted_iota(jnp.int32, (rows, 2 * rows), 0)
    query_row = lax.broadcasted_iota(jnp.int32, (rows, 2 * rows), 1)
    ahead = key_row - jnp.where(query_row < rows, query_row, query_row - rows)
    parts = []
    for slot in range(slots):
        piece = scores[slot * rows : (slot + 1) * rows]
        parts.append(jnp.where(ahead <= places[0] - places[1 + slot], piece, -1e30))
    return parts


def forward_kernel(places, q_ref, *refs):
    slots = (len(refs) - 2) // 2
    key_refs, value_refs = refs[:slots], refs[slots : 2 * slots]
    out_ref, lse_ref = refs[2 * slots :]
    rows = q_ref.shape[1]
    keys = jnp.concatenate([ref[0] for ref in key_refs], axis=0)
    values = jnp.concatenate([ref[0] for ref in value_refs], axis=0)
    two_queries = stacked_heads(q_ref[0] * 0.125)
    parts = masked_scores(places, keys, two_queries, slots, rows)
    top = jnp.max(parts[0], axis=0, keepdims=True)
    for piece in parts[1:]:
        top = jnp.maximum(top, jnp.max(piece, axis=0, keepdims=True))
    parts = [jnp.exp(piece - top) for piece in parts]
    total = jnp.sum(parts[0], axis=0, keepdims=True)
    for piece in parts[1:]:
        total = total + jnp.sum(piece, axis=0, keepdims=True)
    inverse = 1.0 / total
    probs = jnp.concatenate([(piece * inverse).astype(bf16) for piece in parts], axis=0)
    mixed = dot_tn(values, probs)
    chosen = jnp.concatenate([mixed[:HEAD, :rows], mixed[HEAD:, rows:]], axis=0)
    out_ref[0] = chosen.T.astype(bf16)
    lse_ref[0, 0] = top + jnp.log(total)


def backward_kernel(places, q_ref, grad_ref, lse_ref, *refs):
    slots = (len(refs) - 3) // 2
    key_refs, value_refs = refs[:slots], refs[slots : 2 * slots]
    dq_ref, dk_ref, dv_ref = refs[2 * slots :]
    rows = q_ref.shape[1]
    keys = jnp.concatenate([ref[0] for ref in key_refs], axis=0)
    values = jnp.concatenate([ref[0] for ref in value_refs], axis=0)
    two_queries = stacked_heads(q_ref[0] * 0.125)
    two_grads = stacked_heads(grad_ref[0])
    lse = lse_ref[0, 0]
    parts = [jnp.exp(piece - lse) for piece in masked_scores(places, keys, two_queries, slots, rows)]
    prob_grad = dot_nt(values, two_grads)
    delta = jnp.zeros_like(lse)
    for slot in range(slots):
        delta = delta + jnp.sum(
            parts[slot] * prob_grad[slot * rows : (slot + 1) * rows], axis=0, keepdims=True
        )
    score_grad = jnp.concatenate(
        [
            (parts[slot] * (prob_grad[slot * rows : (slot + 1) * rows] - delta)).astype(bf16)
            for slot in range(slots)
        ],
        axis=0,
    )
    probs = jnp.concatenate([piece.astype(bf16) for piece in parts], axis=0)
    dk_ref[:, 0] = dot(score_grad, two_queries).astype(bf16).reshape(slots, rows, 2 * HEAD)
    dv_ref[:, 0] = dot(probs, two_grads).astype(bf16).reshape(slots, rows, 2 * HEAD)
    mixed = dot_tn(keys, score_grad)
    chosen = jnp.concatenate([mixed[:HEAD, :rows], mixed[HEAD:, rows:]], axis=0) * 0.125
    dq_ref[0] = chosen.T.astype(bf16)


def column_spec(rows, first):
    return pl.BlockSpec((1, rows, 2 * HEAD), lambda s, h, places: (s, 0, first + h))


def kv_specs(rows, slots):
    pairs = HEADS // 2
    keys = [column_spec(rows, pairs)] + [column_spec(rows, 0)] * (slots - 1)
    values = [column_spec(rows, 2 * pairs)] + [column_spec(rows, pairs)] * (slots - 1)
    return keys + values


def attend(places, projected, others):
    seqs, rows, _ = projected.shape
    pairs, slots = HEADS // 2, 1 + len(others)
    lse_spec = pl.BlockSpec((1, 1, 1, 2 * rows), lambda s, h, places: (s, h, 0, 0))
    return pl.pallas_call(
        forward_kernel,
        grid_spec=pltpu.PrefetchScalarGridSpec(
            num_scalar_prefetch=1,
            grid=(seqs, pairs),
            in_specs=[column_spec(rows, 0)] + kv_specs(rows, slots),
            out_specs=[column_spec(rows, 0), lse_spec],
        ),
        out_shape=[
            jax.ShapeDtypeStruct((seqs, rows, HEADS * HEAD), bf16),
            jax.ShapeDtypeStruct((seqs, pairs, 1, 2 * rows), f32),
        ],
        compiler_params=pltpu.CompilerParams(vmem_limit_bytes=56 << 20),
    )(places, projected, projected, *others, projected, *others)


def attend_back(places, projected, others, grad_rows, lse):
    seqs, rows, _ = projected.shape
    pairs, slots = HEADS // 2, 1 + len(others)
    lse_spec = pl.BlockSpec((1, 1, 1, 2 * rows), lambda s, h, places: (s, h, 0, 0))
    slot_spec = pl.BlockSpec((slots, 1, rows, 2 * HEAD), lambda s, h, places: (0, s, 0, h))
    return pl.pallas_call(
        backward_kernel,
        grid_spec=pltpu.PrefetchScalarGridSpec(
            num_scalar_prefetch=1,
            grid=(seqs, pairs),
            in_specs=[column_spec(rows, 0), column_spec(rows, 0), lse_spec] + kv_specs(rows, slots),
            out_specs=[column_spec(rows, 0), slot_spec, slot_spec],
        ),
        out_shape=[
            jax.ShapeDtypeStruct((seqs, rows, HEADS * HEAD), bf16),
            jax.ShapeDtypeStruct((slots, seqs, rows, HEADS * HEAD), bf16),
            jax.ShapeDtypeStruct((slots, seqs, rows, HEADS * HEAD), bf16),
        ],
        compiler_params=pltpu.CompilerParams(vmem_limit_bytes=56 << 20),
    )(places, projected, grad_rows, lse, projected, *others, projected, *others)


def gather_shards(shard):
    depth, place = lax.axis_size("z"), lax.axis_index("z")
    found = jnp.stack([shard] + [swap(shard, "z", step) for step in range(1, depth)])
    line = jnp.stack([pick(found, slot ^ place) for slot in range(depth)])
    whole = lax.all_gather(line, PLANE, axis=1, tiled=True)
    return whole.reshape(-1, shard.shape[1])


def finish_over_z(line):
    depth, place = lax.axis_size("z"), lax.axis_index("z")
    total = pick(line, place).astype(f32)
    for step in range(1, depth):
        total = total + swap(pick(line, place ^ step), "z", step).astype(f32)
    return total


def scatter_sum(partial):
    depth = lax.axis_size("z")
    line = lax.psum_scatter(
        partial.reshape(depth, -1, partial.shape[1]), PLANE, scatter_dimension=1, tiled=True
    )
    return finish_over_z(line)


def plane_steps():
    tall, wide = lax.axis_size("y"), lax.axis_size("x")
    return [(core, down, along) for core in (0, 1) for down in range(tall) for along in range(wide)]


def gather_rows(own):
    tall, wide = lax.axis_size("y"), lax.axis_size("x")
    near = {(0, 0): own}
    if tall == 2 and wide == 2:
        near[0, 1] = swap(own, "x", 1)
        near[1, 0] = swap(own, "y", 1)
        near[1, 1] = jnp.concatenate([swap(near[1, 0][:1], "x", 1), swap(near[0, 1][1:], "y", 1)])
    else:
        for down in range(tall):
            for along in range(wide):
                value = swap(own, "y", down) if down else own
                near[down, along] = swap(value, "x", along) if along else value
    far = {place: swap(value, "c", 1) for place, value in near.items()}
    found = [(far if core else near)[down, along] for core, down, along in plane_steps()]
    return found[1:]


def scatter_rows(terms):
    tall, wide = lax.axis_size("y"), lax.axis_size("x")
    half = tall * wide
    chip = (terms[:half].astype(f32) + swap(terms[half:], "c", 1).astype(f32)).astype(bf16)
    chip = chip.reshape((tall, wide) + terms.shape[1:])

    def over(value, axis):
        total = value[0].astype(f32)
        for step in range(1, value.shape[0]):
            total = total + swap(value[step], axis, step).astype(f32)
        return total.astype(bf16)

    first = over(over(jnp.swapaxes(chip[:, :, :1], 0, 1), "x"), "y")
    second = over(over(chip[:, :, 1:], "y"), "x")
    return jnp.concatenate([first, second])


def scatter_sum_split(left, right):
    depth, tall, wide = lax.axis_size("z"), lax.axis_size("y"), lax.axis_size("x")
    spot_y, spot_x, spot_c = lax.axis_index("y"), lax.axis_index("x"), lax.axis_index("c")

    def over(value, axis, spot):
        dim = value.ndim - 3
        total = pick(value, spot, dim).astype(f32)
        for step in range(1, lax.axis_size(axis)):
            total = total + swap(pick(value, spot ^ step, dim), axis, step).astype(f32)
        return total.astype(bf16)

    halves = []
    for value, order in ((left, "xy"), (right, "yx")):
        value = value.reshape(depth, tall, wide, 2, -1, value.shape[1])
        value = over(value, "c", spot_c)
        if order == "xy":
            value = over(over(value, "x", spot_x), "y", spot_y)
        else:
            value = over(over(jnp.swapaxes(value, 1, 2), "y", spot_y), "x", spot_x)
        halves.append(value)
    return finish_over_z(jnp.concatenate(halves, axis=-1))


def per_device(
    patches, w_in, b_in, g_one, s_one, w_qkv, w_out, b_out, g_two, s_two, w_up, b_up, w_down, b_down,
    cotangent,
):
    seqs, rows, in_width = patches.shape
    width = w_out.shape[1]
    ff = w_up.shape[1]
    tall, wide = lax.axis_size("y"), lax.axis_size("x")
    devices = lax.axis_size("z") * tall * wide * 2
    spot = (lax.axis_index("y") * wide + lax.axis_index("x")) * 2 + lax.axis_index("c")
    steps = np.array([(down * wide + along) * 2 + core for core, down, along in plane_steps()])
    places = jnp.concatenate([spot[None], spot ^ jnp.asarray(steps, jnp.int32)]) * rows

    vectors = (b_in, g_one, s_one, b_out, g_two, s_two, b_down, b_up)
    small = b_in.shape[0]
    packed = jnp.concatenate(vectors)
    extra = jnp.zeros((8, width), bf16).at[0, : packed.shape[0]].set(packed)

    in_rows = w_in.shape[0]
    half = in_rows // 2
    first = gather_shards(jnp.concatenate([w_in[:half], extra]))
    second = gather_shards(w_in[half:])
    middle = gather_shards(jnp.concatenate([w_qkv, w_out], axis=1))
    up_all = gather_shards(w_up)
    down_all = gather_shards(w_down)
    first = first.reshape(devices, half + 8, width)
    in_all = jnp.concatenate(
        [first[:, :half], second.reshape(devices, half, width)], axis=1
    ).reshape(in_width, width)
    vec = first[:, half, : packed.shape[0]].astype(f32)
    vec_small = vec[:, : 7 * small].reshape(devices, 7, small).transpose(1, 0, 2).reshape(7, width)
    all_b_in, gain_one, shift_one, all_b_out, gain_two, shift_two, all_b_down = vec_small
    all_b_up = vec[:, 7 * small :].reshape(ff)
    qkv_all, out_all = middle[:, : 3 * width], middle[:, 3 * width :]

    flat = patches.reshape(seqs * rows, in_width)
    h_zero = dot(flat, in_all) + all_b_in
    n_one, normed_one, inverse_one = norm_forward(h_zero, gain_one, shift_one)
    a_one = n_one.astype(bf16)
    projected = dot(a_one, qkv_all).astype(bf16).reshape(seqs, rows, 3 * width)
    others = gather_rows(projected[:, :, width:])
    attended, lse = attend(places, projected, others)
    attended = attended.reshape(seqs * rows, width)
    h_one = h_zero + dot(attended, out_all) + all_b_out
    n_two, normed_two, inverse_two = norm_forward(h_one, gain_two, shift_two)
    a_two = n_two.astype(bf16)
    pre_act = dot(a_two, up_all) + all_b_up
    gelu_out, gelu_slope = gelu_pair(pre_act)
    hidden = gelu_out.astype(bf16)
    result = h_one + dot(hidden, down_all) + all_b_down
    block_out = result.astype(bf16).reshape(seqs, rows, width)

    cot = cotangent.reshape(seqs * rows, width)
    cot_float = cot.astype(f32)
    grad_b_down = jnp.sum(cot_float, axis=0)
    grad_w_down = scatter_sum(dot_tn(hidden, cot).astype(bf16))
    pre_grad = dot_nt(cot, down_all) * gelu_slope
    grad_b_up = jnp.sum(pre_grad, axis=0)
    up_grad = pre_grad.astype(bf16)
    grad_w_up = scatter_sum(dot_tn(a_two, up_grad).astype(bf16))
    two_grad = dot_nt(up_grad, up_all)
    norm_grad, grad_g_two, grad_s_two = norm_backward(two_grad, normed_two, inverse_two, gain_two)
    stream_one = cot_float + norm_grad
    grad_b_out = jnp.sum(stream_one, axis=0)
    out_grad = stream_one.astype(bf16)
    attended_grad = dot_nt(out_grad, out_all).astype(bf16).reshape(seqs, rows, width)
    dq, dk, dv = attend_back(places, projected, others, attended_grad, lse)
    dkv = scatter_rows(jnp.concatenate([dk, dv], axis=-1))
    projected_grad = jnp.concatenate([dq, dkv], axis=-1).reshape(seqs * rows, 3 * width)
    grad_middle = scatter_sum(
        jnp.concatenate(
            [
                dot_tn(a_one, projected_grad).astype(bf16),
                dot_tn(attended, out_grad).astype(bf16),
            ],
            axis=1,
        )
    )
    one_grad = dot_nt(projected_grad, qkv_all)
    norm_grad, grad_g_one, grad_s_one = norm_backward(one_grad, normed_one, inverse_one, gain_one)
    stream_zero = stream_one + norm_grad
    grad_b_in = jnp.sum(stream_zero, axis=0)
    zero_grad = stream_zero.astype(bf16)

    vec_grads = jnp.stack(
        [grad_b_in, grad_g_one, grad_s_one, grad_b_out, grad_g_two, grad_s_two, grad_b_down]
    )
    vec_grads = vec_grads.reshape(7, devices, small).transpose(1, 0, 2).reshape(devices, 7 * small)
    vec_grads = jnp.concatenate([vec_grads, grad_b_up.reshape(devices, -1)], axis=1).astype(bf16)
    tail = jnp.zeros((devices, 8, width), bf16).at[:, 0, : vec_grads.shape[1]].set(vec_grads)
    column = width // 2
    in_halves = []
    for start in (0, column):
        part = dot_tn(flat, zero_grad[:, start : start + column]).astype(bf16)
        part = part.reshape(devices, in_rows, column)
        part = jnp.concatenate([part, tail[:, :, start : start + column]], axis=1)
        in_halves.append(part.reshape(devices * (in_rows + 8), column))
    grad_in = scatter_sum_split(*in_halves)
    grad_patches = dot_nt(zero_grad, in_all).reshape(seqs, rows, in_width)

    vec_own = grad_in[in_rows]
    small_grads = [vec_own[index * small : (index + 1) * small] for index in range(7)]
    grad_b_up = vec_own[7 * small : 7 * small + b_up.shape[0]]
    return (
        block_out,
        grad_patches,
        grad_in[:in_rows],
        small_grads[0],
        small_grads[1],
        small_grads[2],
        grad_middle[:, : 3 * width],
        grad_middle[:, 3 * width :],
        small_grads[3],
        small_grads[4],
        small_grads[5],
        grad_w_up,
        grad_b_up,
        grad_w_down,
        small_grads[6],
    )


def solution(mesh):
    depth, plane = mesh.shape["dp"], mesh.shape["ctx"]
    side = math.isqrt(plane // 2)
    fine = Mesh(mesh.devices.reshape(depth, plane // 2 // side, side, 2), ALL)
    matrix, vector, rows = P(ALL, None), P(ALL), P("z", PLANE, None)
    weights = (
        matrix, vector, vector, vector, matrix, matrix, vector, vector, vector, matrix, vector,
        matrix, vector,
    )
    return jax.shard_map(
        per_device,
        mesh=fine,
        in_specs=(rows,) + weights + (rows,),
        out_specs=(rows, rows) + weights,
        check_vma=False,
    )
```

```python
import math

import jax
import jax.numpy as jnp
import numpy as np
from jax import lax
from jax.experimental import pallas as pl
from jax.experimental.pallas import tpu as pltpu
from jax.sharding import Mesh
from jax.sharding import PartitionSpec as P

HEADS = 12
HEAD = 64

eps_norm = 1e-05
gelu_coef = 0.7978845608028654
PLANE = ("y", "x", "c")
ALL = ("z", "y", "x", "c")
bf16 = jnp.bfloat16
f32 = jnp.float32


def norm_forward(stream, gain, shift):
    row_mean = jnp.mean(stream, axis=-1, keepdims=True)
    centered = stream - row_mean
    variance = jnp.mean(centered * centered, axis=-1, keepdims=True)
    inverse = lax.rsqrt(variance + eps_norm)
    normed = centered * inverse
    return (normed * gain + shift, normed, inverse)


def norm_backward(upstream, normed, inverse, gain):
    scaled = upstream * gain
    row_inner = jnp.mean(scaled, axis=-1, keepdims=True)
    row_corr = jnp.mean(scaled * normed, axis=-1, keepdims=True)
    stream_grad = inverse * (scaled - row_inner - normed * row_corr)
    return (stream_grad, jnp.sum(upstream * normed, axis=0), jnp.sum(upstream, axis=0))


def gelu_pair(pre_act):
    tanh_val = jnp.tanh(gelu_coef * (pre_act + 0.044715 * pre_act * pre_act * pre_act))
    gelu_out = 0.5 * pre_act * (1.0 + tanh_val)
    gelu_slope = 0.5 * (1.0 + tanh_val) + 0.5 * pre_act * (
        1.0 - tanh_val * tanh_val
    ) * gelu_coef * (1.0 + 3.0 * 0.044715 * pre_act * pre_act)
    return (gelu_out, gelu_slope)


def dot(left, right):
    return jnp.dot(left, right, preferred_element_type=f32)


def dot_nt(left, right):
    return lax.dot_general(left, right, (((1,), (1,)), ((), ())), preferred_element_type=f32)


def dot_tn(left, right):
    return lax.dot_general(left, right, (((0,), (0,)), ((), ())), preferred_element_type=f32)


def swap(value, axis, step):
    size = lax.axis_size(axis)
    return lax.ppermute(value, axis, [(place, place ^ step) for place in range(size)])


def after(value, *others):
    return lax.optimization_barrier((value,) + others)[0]


def pick(value, index, dim=0):
    return lax.dynamic_index_in_dim(value, index, dim, keepdims=False)


def stacked_heads(block):
    lane = lax.broadcasted_iota(jnp.int32, block.shape, 1)
    zero = jnp.zeros_like(block)
    return jnp.concatenate(
        [jnp.where(lane < HEAD, block, zero), jnp.where(lane < HEAD, zero, block)], axis=0
    )


def masked_scores(places, keys, two_queries, slots, rows):
    scores = dot_nt(keys, two_queries)
    key_row = lax.broadcasted_iota(jnp.int32, (rows, 2 * rows), 0)
    query_row = lax.broadcasted_iota(jnp.int32, (rows, 2 * rows), 1)
    ahead = key_row - jnp.where(query_row < rows, query_row, query_row - rows)
    parts = []
    for slot in range(slots):
        piece = scores[slot * rows : (slot + 1) * rows]
        parts.append(jnp.where(ahead <= places[0] - places[1 + slot], piece, -1e30))
    return parts


def forward_kernel(places, q_ref, *refs):
    slots = (len(refs) - 2) // 2
    key_refs, value_refs = refs[:slots], refs[slots : 2 * slots]
    out_ref, lse_ref = refs[2 * slots :]
    rows = q_ref.shape[1]
    keys = jnp.concatenate([ref[0] for ref in key_refs], axis=0)
    values = jnp.concatenate([ref[0] for ref in value_refs], axis=0)
    two_queries = stacked_heads(q_ref[0] * 0.125)
    parts = masked_scores(places, keys, two_queries, slots, rows)
    top = jnp.max(parts[0], axis=0, keepdims=True)
    for piece in parts[1:]:
        top = jnp.maximum(top, jnp.max(piece, axis=0, keepdims=True))
    parts = [jnp.exp(piece - top) for piece in parts]
    total = jnp.sum(parts[0], axis=0, keepdims=True)
    for piece in parts[1:]:
        total = total + jnp.sum(piece, axis=0, keepdims=True)
    inverse = 1.0 / total
    probs = jnp.concatenate([(piece * inverse).astype(bf16) for piece in parts], axis=0)
    mixed = dot_tn(values, probs)
    chosen = jnp.concatenate([mixed[:HEAD, :rows], mixed[HEAD:, rows:]], axis=0)
    out_ref[0] = chosen.T.astype(bf16)
    lse_ref[0, 0] = top + jnp.log(total)


def backward_kernel(places, q_ref, grad_ref, lse_ref, *refs):
    slots = (len(refs) - 5) // 2
    key_refs, value_refs = refs[:slots], refs[slots : 2 * slots]
    dq_ref, dk_near, dk_far, dv_near, dv_far = refs[2 * slots :]
    rows = q_ref.shape[1]
    keys = jnp.concatenate([ref[0] for ref in key_refs], axis=0)
    values = jnp.concatenate([ref[0] for ref in value_refs], axis=0)
    two_queries = stacked_heads(q_ref[0] * 0.125)
    two_grads = stacked_heads(grad_ref[0])
    lse = lse_ref[0, 0]
    parts = [jnp.exp(piece - lse) for piece in masked_scores(places, keys, two_queries, slots, rows)]
    prob_grad = dot_nt(values, two_grads)
    delta = jnp.zeros_like(lse)
    for slot in range(slots):
        delta = delta + jnp.sum(
            parts[slot] * prob_grad[slot * rows : (slot + 1) * rows], axis=0, keepdims=True
        )
    score_grad = jnp.concatenate(
        [
            (parts[slot] * (prob_grad[slot * rows : (slot + 1) * rows] - delta)).astype(bf16)
            for slot in range(slots)
        ],
        axis=0,
    )
    probs = jnp.concatenate([piece.astype(bf16) for piece in parts], axis=0)
    half = slots // 2
    key_grad = dot(score_grad, two_queries).astype(bf16).reshape(slots, rows, 2 * HEAD)
    value_grad = dot(probs, two_grads).astype(bf16).reshape(slots, rows, 2 * HEAD)
    dk_near[:, 0], dk_far[:, 0] = key_grad[:half], key_grad[half:]
    dv_near[:, 0], dv_far[:, 0] = value_grad[:half], value_grad[half:]
    mixed = dot_tn(keys, score_grad)
    chosen = jnp.concatenate([mixed[:HEAD, :rows], mixed[HEAD:, rows:]], axis=0) * 0.125
    dq_ref[0] = chosen.T.astype(bf16)


def column_spec(rows, first):
    return pl.BlockSpec((1, rows, 2 * HEAD), lambda s, h, places: (s, 0, first + h))


def kv_specs(rows, slots):
    pairs = HEADS // 2
    keys = [column_spec(rows, pairs)] + [column_spec(rows, 0)] * (slots - 1)
    values = [column_spec(rows, 2 * pairs)] + [column_spec(rows, pairs)] * (slots - 1)
    return keys + values


def attend(places, projected, others):
    seqs, rows, _ = projected.shape
    pairs, slots = HEADS // 2, 1 + len(others)
    lse_spec = pl.BlockSpec((1, 1, 1, 2 * rows), lambda s, h, places: (s, h, 0, 0))
    return pl.pallas_call(
        forward_kernel,
        grid_spec=pltpu.PrefetchScalarGridSpec(
            num_scalar_prefetch=1,
            grid=(seqs, pairs),
            in_specs=[column_spec(rows, 0)] + kv_specs(rows, slots),
            out_specs=[column_spec(rows, 0), lse_spec],
        ),
        out_shape=[
            jax.ShapeDtypeStruct((seqs, rows, HEADS * HEAD), bf16),
            jax.ShapeDtypeStruct((seqs, pairs, 1, 2 * rows), f32),
        ],
        compiler_params=pltpu.CompilerParams(vmem_limit_bytes=56 << 20),
    )(places, projected, projected, *others, projected, *others)


def attend_back(places, projected, others, grad_rows, lse):
    seqs, rows, _ = projected.shape
    pairs, slots = HEADS // 2, 1 + len(others)
    lse_spec = pl.BlockSpec((1, 1, 1, 2 * rows), lambda s, h, places: (s, h, 0, 0))
    half = slots // 2
    slot_spec = pl.BlockSpec((half, 1, rows, 2 * HEAD), lambda s, h, places: (0, s, 0, h))
    return pl.pallas_call(
        backward_kernel,
        grid_spec=pltpu.PrefetchScalarGridSpec(
            num_scalar_prefetch=1,
            grid=(seqs, pairs),
            in_specs=[column_spec(rows, 0), column_spec(rows, 0), lse_spec] + kv_specs(rows, slots),
            out_specs=[column_spec(rows, 0)] + [slot_spec] * 4,
        ),
        out_shape=[jax.ShapeDtypeStruct((seqs, rows, HEADS * HEAD), bf16)]
        + [jax.ShapeDtypeStruct((half, seqs, rows, HEADS * HEAD), bf16)] * 4,
        compiler_params=pltpu.CompilerParams(vmem_limit_bytes=56 << 20),
    )(places, projected, grad_rows, lse, projected, *others, projected, *others)


def gather_line(shard):
    depth, place = lax.axis_size("z"), lax.axis_index("z")
    found = jnp.stack([shard] + [swap(shard, "z", step) for step in range(1, depth)])
    return jnp.stack([pick(found, slot ^ place) for slot in range(depth)])


def gather_plane(line):
    return lax.all_gather(line, PLANE, axis=1, tiled=True).reshape(-1, line.shape[2])


def finish_over_z(line):
    depth, place = lax.axis_size("z"), lax.axis_index("z")
    total = pick(line, place).astype(f32)
    for step in range(1, depth):
        total = total + swap(pick(line, place ^ step), "z", step).astype(f32)
    return total


def scatter_plane(partial):
    depth, width = lax.axis_size("z"), partial.shape[2]
    return lax.psum_scatter(
        partial.reshape(depth, -1, width), PLANE, scatter_dimension=1, tiled=True
    )


def plane_steps():
    tall, wide = lax.axis_size("y"), lax.axis_size("x")
    return [(core, down, along) for core in (0, 1) for down in range(tall) for along in range(wide)]


def gather_rows(own):
    tall, wide = lax.axis_size("y"), lax.axis_size("x")
    near = {(0, 0): own}
    if tall == 2 and wide == 2:
        near[0, 1] = swap(own, "x", 1)
        near[1, 0] = swap(own, "y", 1)
        near[1, 1] = jnp.concatenate([swap(near[1, 0][:1], "x", 1), swap(near[0, 1][1:], "y", 1)])
    else:
        for down in range(tall):
            for along in range(wide):
                value = swap(own, "y", down) if down else own
                near[down, along] = swap(value, "x", along) if along else value
    far = {place: swap(value, "c", 1) for place, value in near.items()}
    found = [(far if core else near)[down, along] for core, down, along in plane_steps()]
    return found[1:]


def add(*terms):
    total = terms[0].astype(f32)
    for term in terms[1:]:
        total = total + term.astype(f32)
    return total


def reduce_near(terms, order):
    def take(value, step, axis):
        return value[step] if axis == "y" or value.ndim < terms[0].ndim else value[:, step]

    inner = [take(value, 0, order[0]) for value in terms]
    for step in range(1, lax.axis_size(order[0])):
        send = add(*[take(value, step, order[0]) for value in terms]).astype(bf16)
        inner.append(swap(send, order[0], step))
    last = [value[0] for value in inner]
    for step in range(1, lax.axis_size(order[1])):
        send = add(*[value[step] for value in inner]).astype(bf16)
        last.append(swap(send, order[1], step))
    return add(*last)


def scatter_rows(near, far, order):
    shape = (lax.axis_size("y"), lax.axis_size("x")) + near.shape[1:]
    return reduce_near([near.reshape(shape), swap(far, "c", 1).reshape(shape)], order).astype(bf16)


def z_line(chunk):
    return jnp.stack([chunk] + [swap(chunk, "z", step) for step in range(1, lax.axis_size("z"))])


def gather_weights(shard, middle, ff, turned):
    line = z_line(shard)
    middle_line = gather_line(after(middle, line))
    along, down = swap(line, "x", 1), swap(line, "y", 1)
    far = [swap(line, "c", 1)]
    along, down = after((along, down), middle_line, turned, *far)
    half = (shard.shape[0] - 8) // 2
    across = [swap(down[:, :half], "x", 1), swap(along[:, half:], "y", 1)]
    far += [swap(along, "c", 1), swap(down, "c", 1)]
    ff_line = gather_line(after(ff, along, down, *across))
    far += [swap(value, "c", 1) for value in across]
    return [line, along, down, *across, *far], after(middle_line, along, down), ff_line


def chip_table():
    depth = lax.axis_size("z")
    own = (lax.axis_index("z") * 2 + lax.axis_index("y")) * 2 + lax.axis_index("x")
    steps = jnp.arange(depth * 4, dtype=jnp.int32)
    return jnp.concatenate([steps ^ own, lax.axis_index("c")[None]]).astype(jnp.int32)


def pack_kernel(*refs):
    weight, out_ref = refs[0], refs[-1]
    rows = weight.shape[0]
    out_ref[:rows] = weight[...]
    out_ref[rows:] = jnp.zeros((out_ref.shape[0] - rows, out_ref.shape[1]), out_ref.dtype)
    for place, ref in enumerate(refs[1:-1]):
        out_ref[rows + place : rows + place + 1, : ref.shape[1]] = ref[...]


def pack(weight, vectors):
    return pl.pallas_call(
        pack_kernel,
        out_shape=jax.ShapeDtypeStruct((weight.shape[0] + 8, weight.shape[1]), weight.dtype),
        name="pack",
    )(weight, *[vector[None] for vector in vectors])


def piece_specs(pieces):
    return [pl.BlockSpec((1,) + value.shape[1:], lambda d, table: (d, 0, 0)) for value in pieces]


def chip_weight(refs, chip, rows, core):
    def shard(side):
        if chip < 3:
            return side[chip][0, :rows]
        return jnp.concatenate([side[3][0], side[4][0, : rows // 2]], axis=0)

    near, far = shard(refs[:5]), shard(refs[5:10])
    first = jnp.where(core == 0, near, far)
    second = jnp.where(core == 0, far, near)
    return jnp.concatenate([first, second], axis=0)


def chip_lanes(table, chip, lanes):
    place = table[pl.program_id(0) * 4 + chip]
    return pl.ds(pl.multiple_of((place % 4) * lanes, 128), lanes)


def enter_kernel(rows, cells, table, flat_ref, *refs):
    out_ref = refs[-1]

    @pl.when(pl.program_id(0) == 0)
    def _():
        out_ref[...] = jnp.zeros_like(out_ref)

    total = out_ref[...]
    for chip in range(4):
        left = flat_ref[:, chip_lanes(table, chip, 2 * rows)]
        total = total + dot(left, chip_weight(refs, chip, rows, table[cells]))
    out_ref[...] = total


def leave_kernel(rows, cells, table, grad_ref, *refs):
    out_ref = refs[-1]
    for chip in range(4):
        right = chip_weight(refs, chip, rows, table[cells])
        out_ref[:, chip_lanes(table, chip, 2 * rows)] = dot_nt(grad_ref[...], right)


def enter(table, flat, pieces, rows):
    depth, width = lax.axis_size("z"), pieces[0].shape[2]
    tokens, lanes = flat.shape[0], 8 * rows
    return pl.pallas_call(
        lambda *refs: enter_kernel(rows, depth * 4, *refs),
        grid_spec=pltpu.PrefetchScalarGridSpec(
            num_scalar_prefetch=1,
            grid=(depth,),
            in_specs=[pl.BlockSpec((tokens, lanes), lambda d, table: (0, table[d * 4] // 4))]
            + piece_specs(pieces),
            out_specs=pl.BlockSpec((tokens, width), lambda d, table: (0, 0)),
        ),
        out_shape=jax.ShapeDtypeStruct((tokens, width), f32),
        compiler_params=pltpu.CompilerParams(vmem_limit_bytes=56 << 20),
        name="enter",
    )(table, flat, *pieces)


def leave(table, grad, pieces, rows):
    depth, width = lax.axis_size("z"), grad.shape[1]
    tokens, lanes = grad.shape[0], 8 * rows
    return pl.pallas_call(
        lambda *refs: leave_kernel(rows, depth * 4, *refs),
        grid_spec=pltpu.PrefetchScalarGridSpec(
            num_scalar_prefetch=1,
            grid=(depth,),
            in_specs=[pl.BlockSpec((tokens, width), lambda d, table: (0, 0))] + piece_specs(pieces),
            out_specs=pl.BlockSpec((tokens, lanes), lambda d, table: (0, table[d * 4] // 4)),
        ),
        out_shape=jax.ShapeDtypeStruct((tokens, depth * lanes), f32),
        compiler_params=pltpu.CompilerParams(vmem_limit_bytes=56 << 20),
        name="leave",
    )(table, grad, *pieces)


def turn_pair(flat, chips):
    core = lax.axis_index("c")
    turned = flat.T.reshape(chips, 2, -1, flat.shape[0])
    got = swap(pick(turned, 1 - core, 1), "c", 1)
    return jnp.concatenate([pick(turned, core, 1), got], axis=-1)


def weight_kernel(plans, table, turned_ref, grad_ref, *out_refs):
    columns = out_refs[0].shape[3]
    for half, (chips, out_ref) in enumerate(zip(plans, out_refs)):
        for place, chip in enumerate(chips):
            left = turned_ref[table[pl.program_id(0) * 4 + chip] % 4]
            right = grad_ref[:, half * columns : (half + 1) * columns]
            out_ref[place, 0] = dot(left, right).astype(bf16)


def weight_terms(table, turned, grad, plans):
    depth = lax.axis_size("z")
    tokens, columns = grad.shape[0], grad.shape[1] // 2
    rows = turned.shape[1]
    return pl.pallas_call(
        lambda *refs: weight_kernel(plans, *refs),
        grid_spec=pltpu.PrefetchScalarGridSpec(
            num_scalar_prefetch=1,
            grid=(depth,),
            in_specs=[
                pl.BlockSpec((4, rows, tokens), lambda d, table: (table[d * 4] // 4, 0, 0)),
                pl.BlockSpec(grad.shape, lambda d, table: (0, 0)),
            ],
            out_specs=[pl.BlockSpec((2, 1, rows, columns), lambda d, table: (0, d, 0, 0))] * 2,
        ),
        out_shape=[jax.ShapeDtypeStruct((2, depth, rows, columns), bf16)] * 2,
        compiler_params=pltpu.CompilerParams(vmem_limit_bytes=56 << 20),
        name="weight_terms",
    )(table, turned, grad)


ORDERS = ("xy", "yx")


def send_terms(table, turned, grad):
    grad = jnp.concatenate([grad, swap(grad, "c", 1)], axis=0)
    sent = weight_terms(table, turned, grad, ((1, 3), (2, 3)))
    return grad, sent, [swap(value, order[0], 1) for value, order in zip(sent, ORDERS)]


def finish_terms(keep, got):
    last = [
        swap(add(kept[1], value[1]).astype(bf16), order[1], 1)
        for kept, value, order in zip(keep, got, ORDERS)
    ]
    line = [add(kept[0], value[0], other) for kept, value, other in zip(keep, got, last)]
    line = jnp.concatenate(line, axis=-1)
    total = line[0]
    for step in range(1, lax.axis_size("z")):
        total = total + swap(line[step].astype(bf16), "z", step).astype(f32)
    return total


def ff_kernel(a_ref, cot_ref, h_ref, b_up_ref, b_down_ref, down_ref, up_ref, *refs):
    out_ref, two_ref, b_grad_ref, terms_ref = refs[:4]
    total, turned, down_terms, up_terms, sems = refs[4:]
    step, last = pl.program_id(0), pl.num_programs(0) - 1
    width = a_ref.shape[1]
    down_rows, up_rows = down_ref.shape[1], up_ref.shape[1]

    @pl.when(step == 0)
    def _():
        total[...] = h_ref[...] + b_down_ref[...]
        two_ref[...] = jnp.zeros_like(two_ref)
        turned[...] = a_ref[...].T

    up, down = up_ref[...].reshape(width, width), down_ref[...].reshape(width, width)
    gelu_out, gelu_slope = gelu_pair(dot(a_ref[...], up) + b_up_ref[0])
    hidden = gelu_out.astype(bf16)
    total[...] += dot(hidden, down)
    pre_grad = dot_nt(cot_ref[...], down) * gelu_slope
    b_grad_ref[0] = jnp.sum(pre_grad, axis=0, keepdims=True)
    up_grad = pre_grad.astype(bf16)
    two_ref[...] += dot_nt(up_grad, up)
    down_terms[step] = dot_tn(hidden, cot_ref[...]).astype(bf16).reshape(down_ref.shape)
    up_terms[step] = dot(turned[...], up_grad).astype(bf16).reshape(up_ref.shape)

    def copies(place):
        devices = down_ref.shape[0]
        start = down_rows + place * up_rows
        return (
            pltpu.make_async_copy(
                down_terms.at[place],
                terms_ref.at[pl.ds(place * devices, devices), pl.ds(0, down_rows)],
                sems.at[0, place],
            ),
            pltpu.make_async_copy(
                up_terms.at[place], terms_ref.at[:, pl.ds(start, up_rows)], sems.at[1, place]
            ),
        )

    for place in range(4):

        @pl.when(step == place)
        def _():
            for copy in copies(place):
                copy.start()

    @pl.when(step == last)
    def _():
        out_ref[...] = total[...].astype(bf16)
        for place in range(4):
            for copy in copies(place):
                copy.wait()


def feed_forward(a_two, cot, h_one, b_up, b_down, gathered):
    tokens, width = a_two.shape
    devices, rows, _ = gathered.shape
    steps = 4
    down_rows, up_rows = rows // 2, rows // 2 // steps
    whole = pl.BlockSpec((tokens, width), lambda step: (0, 0))
    line = pl.BlockSpec((1, 1, width), lambda step: (step, 0, 0))
    down_shape, up_shape = (devices // steps, down_rows, width), (devices, up_rows, width)
    return pl.pallas_call(
        ff_kernel,
        grid=(steps,),
        in_specs=[
            whole,
            whole,
            whole,
            line,
            pl.BlockSpec((1, width), lambda step: (0, 0)),
            pl.BlockSpec(down_shape, lambda step: (step, 0, 0)),
            pl.BlockSpec(up_shape, lambda step: (0, steps + step, 0)),
        ],
        out_specs=[whole, whole, line, pl.BlockSpec(memory_space=pl.ANY)],
        out_shape=[
            jax.ShapeDtypeStruct((tokens, width), bf16),
            jax.ShapeDtypeStruct((tokens, width), f32),
            jax.ShapeDtypeStruct((steps, 1, width), f32),
            jax.ShapeDtypeStruct(gathered.shape, bf16),
        ],
        scratch_shapes=[
            pltpu.VMEM((tokens, width), f32),
            pltpu.VMEM((width, tokens), bf16),
            pltpu.VMEM((steps,) + down_shape, bf16),
            pltpu.VMEM((steps,) + up_shape, bf16),
            pltpu.SemaphoreType.DMA((2, steps)),
        ],
        compiler_params=pltpu.CompilerParams(vmem_limit_bytes=56 << 20),
        name="feed_forward",
    )(a_two, cot, h_one, b_up.reshape(steps, 1, width), b_down[None], gathered, gathered)


def terms_kernel(blocks, width, *refs):
    count = len(blocks)
    pairs, tail, out_ref = refs[: 2 * count], refs[2 * count : -1 - count], refs[-1 - count]
    turned = refs[-count:]
    step, group = pl.program_id(0), out_ref.shape[0]

    @pl.when(step == 0)
    def _():
        for left, ref in zip(pairs[::2], turned):
            ref[...] = left[...].T

    start = 0
    for index, block in enumerate(blocks):
        rows = block[0] * group
        left = turned[index][pl.ds(pl.multiple_of(step * rows, 16), rows), :]
        result = dot(left, pairs[2 * index + 1][...]).astype(bf16)
        for place in range(group):
            for column in range(block[1]):
                part = result[place * block[0] : (place + 1) * block[0]]
                out_ref[place, start + column * block[0] : start + (column + 1) * block[0], :] = part[
                    :, column * width : (column + 1) * width
                ]
        start += block[0] * block[1]
    if tail:
        out_ref[:, start:, :] = tail[0][...]


def device_terms(pairs, devices, width, tail=None):
    blocks = [(left.shape[1] // devices, right.shape[1] // width) for left, right in pairs]
    rows = sum(row * block for row, block in blocks) + (0 if tail is None else tail.shape[1])
    steps = 8
    if devices % steps or any(row * (devices // steps) % 16 or row % 8 for row, _ in blocks):
        parts = [by_columns(dot_tn(left, right).astype(bf16), devices, width) for left, right in pairs]
        return jnp.concatenate(parts + ([] if tail is None else [tail]), axis=1)
    group = devices // steps
    operands = [value for pair in pairs for value in pair]
    in_specs = [pl.BlockSpec(value.shape, lambda step: (0, 0)) for value in operands]
    if tail is not None:
        operands.append(tail)
        in_specs.append(pl.BlockSpec((group,) + tail.shape[1:], lambda step: (step, 0, 0)))
    return pl.pallas_call(
        lambda *refs: terms_kernel(blocks, width, *refs),
        grid=(steps,),
        in_specs=in_specs,
        out_specs=pl.BlockSpec((group, rows, width), lambda step: (step, 0, 0)),
        out_shape=jax.ShapeDtypeStruct((devices, rows, width), bf16),
        scratch_shapes=[pltpu.VMEM(left.shape[::-1], bf16) for left, _ in pairs],
        compiler_params=pltpu.CompilerParams(vmem_limit_bytes=56 << 20),
        name="device_terms",
    )(*operands)


def by_columns(value, devices, width):
    value = value.reshape(devices, -1, value.shape[1] // width, width)
    return jnp.swapaxes(value, 1, 2).reshape(devices, -1, width)


def from_columns(value, columns):
    blocks, width = columns // value.shape[1], value.shape[1]
    return jnp.swapaxes(value.reshape(blocks, -1, width), 0, 1).reshape(-1, columns)


def per_device(
    patches, w_in, b_in, g_one, s_one, w_qkv, w_out, b_out, g_two, s_two, w_up, b_up, w_down, b_down,
    cotangent,
):
    seqs, rows, in_width = patches.shape
    width = w_out.shape[1]
    ff = w_up.shape[1]
    tall, wide = lax.axis_size("y"), lax.axis_size("x")
    devices = lax.axis_size("z") * tall * wide * 2
    spot = (lax.axis_index("y") * wide + lax.axis_index("x")) * 2 + lax.axis_index("c")
    steps = np.array([(down * wide + along) * 2 + core for core, down, along in plane_steps()])
    places = jnp.concatenate([spot[None], spot ^ jnp.asarray(steps, jnp.int32)]) * rows

    vectors = (b_in, g_one, s_one, b_out, g_two, s_two, b_down, b_up)
    small, count = b_in.shape[0], b_up.shape[0]

    in_rows = w_in.shape[0]
    half = in_rows // 2
    flat = patches.reshape(seqs * rows, in_width)
    fast = tall == 2 and wide == 2 and (2 * in_rows) % 128 == 0 and half % 16 == 0
    if fast:
        turned = turn_pair(flat, devices // 2)
        middle = jnp.concatenate([w_qkv, w_out], axis=1)
        up_rows = jnp.concatenate([w_up[:, i * width : (i + 1) * width] for i in range(ff // width)])
        pieces, middle, ff_all = gather_weights(
            pack(w_in, vectors), middle, jnp.concatenate([w_down, up_rows]), turned
        )
        table = chip_table()
        bases = [in_rows, in_rows, in_rows, None, half] * 2
        found = [value[:, base:, :count] for value, base in zip(pieces, bases) if base is not None]
        found = jnp.stack(found).reshape(2, 4, -1, 8 * count).transpose(2, 1, 0, 3).reshape(devices, 8 * count)
        own = (lax.axis_index("z") * tall * wide * 2) + spot
        order = jnp.arange(devices)[:, None] ^ own
        chosen = (order == jnp.arange(devices)[None, :]).astype(f32)
        vec = jnp.dot(chosen, found.astype(f32), precision=lax.Precision.HIGHEST)
        vec = vec.reshape(devices, 8, count)
        h_zero = enter(table, flat, pieces, in_rows)
    else:
        extra = jnp.stack([jnp.pad(vector, (0, width - vector.shape[0])) for vector in vectors])
        first = gather_plane(gather_line(w_in[:half])).reshape(devices, half, width)
        second = gather_plane(gather_line(jnp.concatenate([w_in[half:], extra])))
        second = second.reshape(devices, half + 8, width)
        in_all = jnp.concatenate([first, second[:, :half]], axis=1).reshape(in_width, width)
        vec = second[:, half:, :count].astype(f32)
        h_zero = dot(flat, in_all)
        middle = gather_line(jnp.concatenate([w_qkv, w_out], axis=1))
    middle = gather_plane(middle)
    if fast:
        ff_all = gather_plane(after(ff_all, h_zero)).reshape(devices, -1, width)
    else:
        up_all = gather_plane(gather_line(w_up))
        down_all = gather_plane(gather_line(w_down))
    vec_small = vec[:, :7, :small].transpose(1, 0, 2).reshape(7, width)
    all_b_in, gain_one, shift_one, all_b_out, gain_two, shift_two, all_b_down = vec_small
    all_b_up = vec[:, 7].reshape(ff)
    qkv_all, out_all = middle[:, : 3 * width], middle[:, 3 * width :]

    h_zero = h_zero + all_b_in
    n_one, normed_one, inverse_one = norm_forward(h_zero, gain_one, shift_one)
    a_one = n_one.astype(bf16)
    projected = dot(a_one, qkv_all).astype(bf16).reshape(seqs, rows, 3 * width)
    others = gather_rows(projected[:, :, width:])
    attended, lse = attend(places, projected, others)
    attended = attended.reshape(seqs * rows, width)
    h_one = h_zero + dot(attended, out_all) + all_b_out
    n_two, normed_two, inverse_two = norm_forward(h_one, gain_two, shift_two)
    a_two = n_two.astype(bf16)
    cot = cotangent.reshape(seqs * rows, width)
    cot_float = cot.astype(f32)
    grad_b_down = jnp.sum(cot_float, axis=0)
    if fast:
        result, two_grad, grad_b_up, ff_terms = feed_forward(
            a_two, cot, h_one, all_b_up, all_b_down, ff_all
        )
        grad_b_up = grad_b_up.reshape(ff)
    else:
        pre_act = dot(a_two, up_all) + all_b_up
        gelu_out, gelu_slope = gelu_pair(pre_act)
        hidden = gelu_out.astype(bf16)
        result = (h_one + dot(hidden, down_all) + all_b_down).astype(bf16)
        pre_grad = dot_nt(cot, down_all) * gelu_slope
        grad_b_up = jnp.sum(pre_grad, axis=0)
        up_grad = pre_grad.astype(bf16)
        two_grad = dot_nt(up_grad, up_all)
        ff_terms = device_terms([(hidden, cot), (a_two, up_grad)], devices, width)
    block_out = result.reshape(seqs, rows, width)
    ff_sums = scatter_plane(ff_terms)
    down_rows = w_down.shape[0]
    norm_grad, grad_g_two, grad_s_two = norm_backward(two_grad, normed_two, inverse_two, gain_two)
    stream_one = cot_float + norm_grad
    grad_b_out = jnp.sum(stream_one, axis=0)
    out_grad = stream_one.astype(bf16)
    attended_grad = dot_nt(out_grad, out_all).astype(bf16).reshape(seqs, rows, width)
    dq, dk_near, dk_far, dv_near, dv_far = attend_back(
        places, projected, others, attended_grad, lse
    )
    dk = scatter_rows(dk_near, dk_far, "xy")
    dv = scatter_rows(dv_near, dv_far, "yx")
    projected_grad = jnp.concatenate([dq, dk, dv], axis=-1).reshape(seqs * rows, 3 * width)
    one_grad = dot_nt(projected_grad, qkv_all)
    norm_grad, grad_g_one, grad_s_one = norm_backward(one_grad, normed_one, inverse_one, gain_one)
    stream_zero = stream_one + norm_grad
    grad_b_in = jnp.sum(stream_zero, axis=0)
    zero_grad = stream_zero.astype(bf16)

    vec_grads = jnp.stack(
        [grad_b_in, grad_g_one, grad_s_one, grad_b_out, grad_g_two, grad_s_two, grad_b_down]
    )
    vec_grads = vec_grads.reshape(7, devices, small).transpose(1, 0, 2)
    tail = jnp.zeros((devices, 16, width), bf16).at[:, :7, :small].set(vec_grads.astype(bf16))
    tail = tail.at[:, 7, :count].set(grad_b_up.reshape(devices, count).astype(bf16))
    sent = []
    if fast:
        pair_grad, sent, got = send_terms(table, turned, zero_grad)
        keep = weight_terms(table, turned, after(pair_grad, *sent), ((0, 2), (0, 1)))
        sent = list(keep)
    a_later = after(a_one, ff_sums, *sent)
    middle_terms = device_terms(
        [(a_later, projected_grad), (attended, out_grad)], devices, width, tail
    )
    grad_ff = finish_over_z(ff_sums)
    grad_w_down, grad_w_up = grad_ff[:down_rows], from_columns(grad_ff[down_rows:], ff)
    if fast:
        grad_patches = leave(table, after(zero_grad, middle_terms), pieces, in_rows)
        got = after(tuple(got), grad_patches, grad_ff)
        grad_in = finish_terms(keep, got)
    else:
        grad_in = dot_tn(flat, zero_grad).astype(bf16).reshape(devices, -1, width)
        grad_in = finish_over_z(scatter_plane(grad_in))
        grad_patches = dot_nt(zero_grad, in_all)
    grad_patches = grad_patches.reshape(seqs, rows, in_width)
    grad_middle = finish_over_z(scatter_plane(middle_terms))
    out_rows = w_out.shape[0]
    grad_w_qkv = from_columns(grad_middle[: 3 * out_rows], 3 * width)
    grad_w_out = grad_middle[3 * out_rows : 4 * out_rows]
    vec_own = grad_middle[4 * out_rows :]

    small_grads = vec_own[:7, :small]
    grad_b_up = vec_own[7, :count]
    return (
        block_out,
        grad_patches,
        grad_in,
        small_grads[0],
        small_grads[1],
        small_grads[2],
        grad_w_qkv,
        grad_w_out,
        small_grads[3],
        small_grads[4],
        small_grads[5],
        grad_w_up,
        grad_b_up,
        grad_w_down,
        small_grads[6],
    )


def solution(mesh):
    depth, plane = mesh.shape["dp"], mesh.shape["ctx"]
    side = math.isqrt(plane // 2)
    fine = Mesh(mesh.devices.reshape(depth, plane // 2 // side, side, 2), ALL)
    matrix, vector, rows = P(ALL, None), P(ALL), P("z", PLANE, None)
    weights = (
        matrix, vector, vector, vector, matrix, matrix, vector, vector, vector, matrix, vector,
        matrix, vector,
    )
    return jax.shard_map(
        per_device,
        mesh=fine,
        in_specs=(rows,) + weights + (rows,),
        out_specs=(rows, rows) + weights,
        check_vma=False,
    )
```
